512 devices in a mesh: tx: 64 (over x, z), ty: 8 (over y, core).
Axes of the slice: x: 4, y: 4, z: 16, core: 2. Of those that a mesh axis runs over, the one named last changes fastest.
Arguments:
- forcing: float32 [3, 6, 1024, 1024], P(None, None, 'tx', 'ty'), may hold values from -6 to 6
- start_state: float32 [3, 6, 1024, 1024], P(None, None, 'tx', 'ty'), may hold values from -4 to 4
- ice_mask: int32 [1024, 1024], P('tx', 'ty'), may hold values from 0 to 2
- class_ids: int32 [6, 1024, 1024], P(None, 'tx', 'ty'), may hold values from 0 to 15
- eta_table: float32 [16], replicated, may hold values from 0.1 to 10
- friction: float32 [1024, 1024], P('tx', 'ty'), may hold values from 0.3 to 30
Outputs:
- adjoint: float32 [3, 6, 1024, 1024], P(None, None, 'tx', 'ty')
- residual: float32 [3, 6, 1024, 1024], P(None, None, 'tx', 'ty')
The draws below stay inside these ranges and needn't reach their ends.
Inputs may be any that keep to these rules, and one draw needn't show every extreme that they name: `ice_mask`: 0 marks an ocean column, 1 a grounded one, 2 a floating one. `class_ids`: an index into eta_table.
All inputs are finite; a program needn't handle non-finite values.
Results may differ from the reference program's by a relative error of at most 0.00002.
Values sent between devices are 32-bit elements; how exact they have to be, the bound alone decides.
A program may use at most 64 MiB of HBM per device.

```python
import math
import jax
import jax.numpy as jnp
from jax import lax

NZ = 6
NCLASS = 16
SWEEPS = 2
COARSE_SWEEPS = 4
NX = 1024
NY = 1024


def place_ends(result, rng, smallest, largest):
    longest = result.shape.index(max(result.shape))
    spots = []
    for shift in (0, 1):
        where = [jax.random.randint(jax.random.fold_in(rng, axis), (), 0, length) for axis, length in enumerate(result.shape)]
        where[longest] = (where[longest] + shift) % result.shape[longest]
        spots.append(tuple(where))
    return result.at[spots[0]].set(smallest).at[spots[1]].set(largest)


def block_levels(rng, dims, shards, smallest, high):
    def one(position, parts):
        steps = jax.random.uniform(jax.random.fold_in(jax.random.fold_in(rng, 6), position), (parts,), jnp.float32, smallest / len(shards), high / len(shards))
        return jnp.repeat(jnp.exp(steps), dims[position] // parts).reshape((-1,) + (1,) * (len(dims) - position - 1))

    level = one(*shards[0])
    for cut in shards[1:]:
        level = level * one(*cut)
    return level


def noise(stream_key, extent, scale, limit, cuts=(), held_as=jnp.bfloat16):
    factor_of = block_levels(stream_key, extent, cuts, -0.22, 0.18) if cuts else 1.0
    drawn = jax.random.normal(stream_key, extent, jnp.float32) * scale * factor_of
    return jnp.minimum(jnp.maximum(drawn, -limit), limit).astype(held_as)


def setup_inputs(seed: int = 0) -> dict:
    key_list = jax.random.split(jax.random.key(seed), 7)
    forcing = noise(key_list[0], (3, NZ, NX, NY), 1.0, 6.0, ((2, 64), (3, 8)), jnp.float32)
    start_state = noise(key_list[1], (3, NZ, NX, NY), 0.5, 4.0, ((2, 64), (3, 8)), jnp.float32)
    ice_mask = place_ends(jax.random.randint(key_list[2], (NX, NY), 0, 3), jax.random.fold_in(key_list[2], 1), 0, 2).astype(jnp.int32)
    class_ids = place_ends(jax.random.randint(key_list[3], (NZ, NX, NY), 0, NCLASS), jax.random.fold_in(key_list[3], 1), 0, NCLASS - 1).astype(jnp.int32)
    eta_table = jnp.clip(jnp.exp(jax.random.uniform(key_list[4], (NCLASS,), jnp.float32, math.log(0.1), math.log(10.0))), 0.1, 10.0)
    friction = jnp.clip(jnp.exp(math.log(30.0) - 4.6051701 * jax.random.uniform(key_list[5], (NX, NY), jnp.float32) ** block_levels(key_list[5], (NX, NY), ((0, 64), (1, 8)), -0.2, 0.2)), 0.3, 30.0)
    return {"forcing": forcing, "start_state": start_state, "ice_mask": ice_mask, "class_ids": class_ids, "eta_table": eta_table, "friction": friction}


DAMPING = 0.6
VERTICAL = 2.0
REACTION = 0.05


def stencil_terms():
    terms = []
    for step_z in (-1, 0, 1):
        for step_x in (-1, 0, 1):
            for step_y in (-1, 0, 1):
                nonzero_axes = abs(step_z) + abs(step_x) + abs(step_y)
                if nonzero_axes > 0:
                    terms.append((step_z, step_x, step_y, nonzero_axes))
    return terms


def apply_operator(padded, coef_pad, spacing, ocean_weight):
    layers = padded.shape[1]
    width_x = padded.shape[2] - 2
    width_y = padded.shape[3] - 2
    viscosity = coef_pad[:layers]
    active = jnp.broadcast_to(coef_pad[layers], viscosity.shape)
    basal = coef_pad[layers + 1]
    visc_z = jnp.pad(viscosity, ((1, 1), (0, 0), (0, 0)))
    active_z = jnp.pad(active, ((1, 1), (0, 0), (0, 0)))
    field_z = jnp.pad(padded, ((0, 0), (1, 1), (0, 0), (0, 0)))
    visc_mid = viscosity[:, 1:1 + width_x, 1:1 + width_y]
    active_mid = active[:, 1:1 + width_x, 1:1 + width_y]
    coupled = jnp.zeros((3, layers, width_x, width_y), jnp.float32)
    weight_sum = jnp.zeros((3, layers, width_x, width_y), jnp.float32)
    for step_z, step_x, step_y, nonzero_axes in stencil_terms():
        base_weight = (0.25 ** (nonzero_axes - 1)) * (VERTICAL ** abs(step_z)) * (spacing ** (abs(step_x) + abs(step_y)))
        factors = jnp.array([1.0 + abs(step_x), 1.0 + abs(step_y), 1.0 + abs(step_z)], jnp.float32).reshape(3, 1, 1, 1) * base_weight
        z_range = slice(1 + step_z, 1 + step_z + layers)
        x_range = slice(1 + step_x, 1 + step_x + width_x)
        y_range = slice(1 + step_y, 1 + step_y + width_y)
        pair_mean = 0.5 * (visc_mid + visc_z[z_range, x_range, y_range]) * active_mid * active_z[z_range, x_range, y_range]
        links = factors * pair_mean[None]
        coupled = coupled + links * field_z[:, z_range, x_range, y_range]
        weight_sum = weight_sum + links
    layer_ids = lax.broadcasted_iota(jnp.int32, (3, layers, 1, 1), 1)
    comp_ids = lax.broadcasted_iota(jnp.int32, (3, layers, 1, 1), 0)
    bottom = jnp.where((layer_ids == 0) & (comp_ids < 2), 1.0, 0.0).astype(jnp.float32)
    basal_term = bottom * basal[None, None, 1:1 + width_x, 1:1 + width_y]
    diagonal = weight_sum + (REACTION * visc_mid * active_mid + ocean_weight * (1.0 - active_mid))[None] + basal_term
    centre = padded[:, :, 1:1 + width_x, 1:1 + width_y]
    return diagonal * centre - coupled, diagonal


def jacobi_sweep(padded, right_side, coef_pad, spacing, ocean_weight):
    applied, diagonal = apply_operator(padded, coef_pad, spacing, ocean_weight)
    centre = padded[:, :, 1:-1, 1:-1]
    return centre + DAMPING * (right_side - applied) / diagonal


def build_coefficients(class_ids, eta_table, ice_mask, friction):
    levels = lax.broadcasted_iota(jnp.int32, (eta_table.shape[0], 1, 1, 1), 0)
    viscosity = jnp.sum(jnp.where(class_ids[None] == levels, eta_table[:, None, None, None], 0.0), axis=0)
    active = jnp.where(ice_mask != 0, 1.0, 0.0).astype(jnp.float32)
    basal = jnp.where(ice_mask == 1, friction, 0.0)
    return jnp.concatenate([viscosity, active[None], basal[None]], axis=0)


def coarsen_sum(values):
    leading = values.shape[:-2]
    shaped = values.reshape(leading + (values.shape[-2] // 2, 2, values.shape[-1] // 2, 2))
    return jnp.sum(shaped, axis=(-3, -1))


def coarse_coefficients(coefficients):
    layers = coefficients.shape[0] - 2
    summed = coarsen_sum(coefficients)
    return jnp.concatenate([summed[:layers], 0.25 * summed[layers:layers + 1], summed[layers + 1:]], axis=0)


def refine(values):
    return jnp.repeat(jnp.repeat(values, 2, axis=-2), 2, axis=-1)


def pad_grid(values):
    return jnp.pad(values, ((0, 0), (0, 0), (1, 1), (1, 1)))


def reference(forcing, start_state, ice_mask, class_ids, eta_table, friction):
    coefficients = build_coefficients(class_ids, eta_table, ice_mask, friction)
    coef_pad = jnp.pad(coefficients, ((0, 0), (1, 1), (1, 1)))
    iterate = start_state
    for sweep_index in range(SWEEPS):
        iterate = jacobi_sweep(pad_grid(iterate), forcing, coef_pad, 1.0, 1.0)
    applied, unused_diag = apply_operator(pad_grid(iterate), coef_pad, 1.0, 1.0)
    fine_residual = forcing - applied
    coarse_rhs = coarsen_sum(fine_residual)
    coarse_pad = jnp.pad(coarse_coefficients(coefficients), ((0, 0), (1, 1), (1, 1)))
    correction = jnp.zeros_like(coarse_rhs)
    for sweep_index in range(COARSE_SWEEPS):
        correction = jacobi_sweep(pad_grid(correction), coarse_rhs, coarse_pad, 0.5, 4.0)
    iterate = iterate + refine(correction)
    for sweep_index in range(SWEEPS):
        iterate = jacobi_sweep(pad_grid(iterate), forcing, coef_pad, 1.0, 1.0)
    applied, unused_diag = apply_operator(pad_grid(iterate), coef_pad, 1.0, 1.0)
    return iterate, forcing - applied
```

```python
import functools

import jax
import jax.numpy as jnp
from jax import lax
from jax.experimental import pallas as pl
from jax.experimental.pallas import tpu as pltpu
from jax.sharding import PartitionSpec as P

DAMPING = 0.6
REACTION = 0.05
NZ = 6
LX = 16
FO = 4
CO = 12
KO = 6
FROWS = LX + 2 * FO
CROWS = LX + 2 * CO
KROWS = LX // 2 + 2 * KO
PACK_A_OWN, PACK_A = 32, 48
PACK_B_OWN, PACK_B = 24, 40


def lanes():
    return lax.broadcasted_iota(jnp.int32, (8, 128), 1)


def layers():
    return lax.broadcasted_iota(jnp.int32, (8, 128), 0)


def rows(low, high, step, body):
    def run(i, carry):
        for k in range(step):
            body(low + i * step + k)
        return carry

    lax.fori_loop(0, (high - low) // step, run, 0)


def along_y(main, halo, weight, shift):
    m1, h1 = pltpu.roll(main, shift, 1), pltpu.roll(halo, shift, 1)
    m2, h2 = pltpu.roll(main, 128 - shift, 1), pltpu.roll(halo, 128 - shift, 1)
    first, last = lanes() < shift, lanes() >= 128 - shift
    near_main = jnp.where(first, h1, m1) + jnp.where(last, h2, m2)
    near_halo = jnp.where(first, m1, h1) + jnp.where(last, m2, h2)
    return main + weight * near_main, halo + weight * near_halo


def along_z(tile, weight):
    return tile + weight * (pltpu.roll(tile, 1, 0) + pltpu.roll(tile, 7, 0))


def pack(items):
    packed = pltpu.roll(items[0], 16, 1)
    for j in range(1, len(items)):
        packed = jnp.where(lanes() >= 32 * j, pltpu.roll(items[j], 16 + 32 * j, 1), packed)
    return packed


def unpack(from_left, from_right, count):
    both = jnp.where(lanes() % 32 < 16, from_left, from_right)
    return [pltpu.roll(both, 112 - 32 * j, 1) for j in range(count)]


def kernel(
    ntx, nty,
    eta, forcing, start, mask, classes, friction, out_u, out_r,
    u, f, cf, a, av, d, inv, ub, g, ka, kav, kv, kd, kinv, kr, kc,
    pa, pal, par, pb, pbl, pbr, send, recv,
):
    tx, ty = lax.axis_index("tx"), lax.axis_index("ty")
    up, down = lax.rem(tx + 1, ntx), lax.rem(tx + ntx - 1, ntx)
    right, left = lax.rem(ty + 1, nty), lax.rem(ty + nty - 1, nty)
    barrier = pltpu.get_barrier_semaphore()
    for where in ({"tx": up}, {"tx": down}, {"ty": right}, {"ty": left}):
        pl.semaphore_signal(barrier, inc=1, device_id=where, device_id_type=pl.DeviceIdType.MESH)

    zero = jnp.zeros((LX, 128), jnp.float32)
    for c in range(3):
        for z in range(8):
            u[0, c, FO : FO + LX, z, :] = start[c, z] if z < NZ else zero
            f[0, c, FO : FO + LX, z, :] = forcing[c, z] if z < NZ else zero
    for z in range(NZ):
        ids = classes[z]
        visc = jnp.zeros((LX, 128), jnp.float32)
        for k in range(eta.shape[0]):
            visc = jnp.where(ids == k, eta[k], visc)
        cf[0, CO : CO + LX, z, :] = visc
    kind = mask[...]
    cf[0, CO : CO + LX, 6, :] = jnp.where(kind != 0, 1.0, 0.0).astype(jnp.float32)
    cf[0, CO : CO + LX, 7, :] = jnp.where(kind == 1, friction[...], 0.0)

    used = [0]

    def copy(src, dst, where):
        k = used[0]
        used[0] += 1
        made = pltpu.make_async_remote_copy(
            src_ref=src, dst_ref=dst, send_sem=send.at[k], recv_sem=recv.at[k],
            device_id=where, device_id_type=pl.DeviceIdType.MESH,
        )
        made.start()
        return made

    def to_both_rows(make, first, count, own):
        top = copy(make(first + own - count, count), make(first - count, count), {"tx": up})
        low = copy(make(first, count), make(first + own, count), {"tx": down})
        return [top, low]

    def to_both_lanes(packed, from_left, from_right, first, count):
        part = pl.ds(first, count)
        return [
            copy(packed.at[part], from_left.at[part], {"ty": right}),
            copy(packed.at[part], from_right.at[part], {"ty": left}),
        ]

    def tri(ref):
        return lambda first, count: ref.at[0, :, pl.ds(first, count)]

    pl.semaphore_wait(barrier, 4)
    x_a = to_both_rows(tri(u), FO, 4, LX)
    x_a += to_both_rows(tri(f), FO, 2, LX)
    x_a += to_both_rows(lambda first, count: cf.at[0, pl.ds(first, count)], CO, 12, LX)

    def pack_u(x, slot):
        pa[slot] = pack([u[0, 0, x + FO], u[0, 1, x + FO], u[0, 2, x + FO], cf[0, x + CO]])

    def pack_f(x, slot):
        pa[slot] = pack([f[0, c, x + FO] for c in range(3)])

    def pack_k(x, slot):
        pa[slot] = pack([cf[0, x + CO + j] for j in range(4)])

    def unpack_u(x, slot):
        got = unpack(pal[slot], par[slot], 4)
        for c in range(3):
            u[1, c, x + FO] = got[c]
        cf[1, x + CO] = got[3]

    def unpack_f(x, slot):
        got = unpack(pal[slot], par[slot], 3)
        for c in range(3):
            f[1, c, x + FO] = got[c]

    def unpack_k(x, slot):
        got = unpack(pal[slot], par[slot], 4)
        for j in range(4):
            cf[1, x + CO + j] = got[j]

    def own_a(do_u, do_f):
        def body(x):
            do_u(x, x)
            do_f(x, x + LX)

        rows(0, LX, 4, body)

    def halo_a(do_u, do_f, do_k):
        for j in range(4):
            do_u(j - 4, 32 + j)
            do_u(LX + j, 36 + j)
        for j in range(2):
            do_f(j - 2, 40 + j)
            do_f(LX + j, 42 + j)
            do_k(4 * j - 12, 44 + j)
            do_k(LX + 4 + 4 * j, 46 + j)

    own_a(pack_u, pack_f)
    y_own = to_both_lanes(pa, pal, par, 0, PACK_A_OWN)
    for made in x_a:
        made.wait_recv()
    halo_a(pack_u, pack_f, pack_k)
    y_halo = to_both_lanes(pa, pal, par, PACK_A_OWN, PACK_A - PACK_A_OWN)
    for made in y_own:
        made.wait_recv()
    own_a(unpack_u, unpack_f)
    for made in y_halo:
        made.wait_recv()
    halo_a(unpack_u, unpack_f, unpack_k)

    in_column = layers() < NZ
    beyond = ((lanes() < 64) & (ty == nty - 1)) | ((lanes() >= 64) & (ty == 0))
    inside = (in_column, in_column & jnp.logical_not(beyond))

    def row_inside(x, count):
        return jnp.logical_not(((x < 0) & (tx == 0)) | ((x >= count) & (tx == ntx - 1)))

    def fine_fields(x):
        for t in range(2):
            tile = cf[t, x + CO]
            keep = inside[t] & row_inside(x, LX)
            active = jnp.where(keep, jnp.broadcast_to(tile[6:7], (8, 128)), 0.0)
            a[t, x + FO] = active
            av[t, x + FO] = active * tile

    def coarse_fields(x):
        for t in range(2):
            tile = cf[t, 2 * x + CO] + cf[t, 2 * x + 1 + CO]
            other = jnp.where(lanes() % 2 == 0, pltpu.roll(tile, 127, 1), pltpu.roll(tile, 1, 1))
            tile = tile + other
            keep = inside[t] & row_inside(x, LX // 2)
            active = jnp.where(keep, 0.25 * jnp.broadcast_to(tile[6:7], (8, 128)), 0.0)
            kv[t, x + KO] = tile
            ka[t, x + KO] = active
            kav[t, x + KO] = active * tile

    def spread(field, low, high, spacing, shift, offset, flags, products):
        def body(x):
            r = x + offset
            for c in range(3):
                weight_y = 0.25 * spacing * (2.0 if c == 1 else 1.0)
                weight_z = 0.5 * (2.0 if c == 2 else 1.0)
                for k, scale in enumerate((flags, products)):
                    tiles = []
                    for t in range(2):
                        s = scale[t, r]
                        tiles.append(s if field is None else s * field[t, c, r])
                    tiles = along_y(tiles[0], tiles[1], weight_y, shift)
                    for t in range(2):
                        g[k, t, c, r] = along_z(tiles[t], weight_z)

        rows(low - 1, high + 1, 2, body)

    def coupled(t, c, r, spacing, flag, visc):
        weight = 0.25 * spacing * (2.0 if c == 0 else 1.0)
        p = g[0, t, c, r] + weight * (g[0, t, c, r - 1] + g[0, t, c, r + 1])
        q = g[1, t, c, r] + weight * (g[1, t, c, r - 1] + g[1, t, c, r + 1])
        return 2.0 * flag * (visc * p + q)

    def diagonals(low, high, spacing, ocean, shift, offset, flags, products, visc, diag, scaled):
        spread(None, low, high, spacing, shift, offset, flags, products)

        def body(x):
            r = x + offset
            for t in range(2):
                tile, flag, product = visc(t, x), flags[t, r], products[t, r]
                basal = jnp.where(layers() == 0, jnp.broadcast_to(tile[7:8], (8, 128)), 0.0)
                base = REACTION * product + ocean * (1.0 - flag)
                for c in range(3):
                    whole = coupled(t, c, r, spacing, flag, tile) + base
                    if c < 2:
                        whole = whole + basal
                    diag[t, c, r] = whole
                    scaled[t, c, r] = DAMPING / (whole - 4.0 * flag * product)

        rows(low, high, 2, body)

    def fine_visc(t, x):
        return cf[t, x + CO]

    def coarse_visc(t, x):
        return kv[t, x + KO]

    def fine_step(field, low, high, finish, tiles=(0, 1)):
        spread(field, low, high, 1.0, 1, FO, a, av)

        def body(x):
            r = x + FO
            for t in tiles:
                flag, visc = a[t, r], cf[t, x + CO]
                for c in range(3):
                    value = field[t, c, r]
                    left_over = f[t, c, r] - d[t, c, r] * value + coupled(t, c, r, 1.0, flag, visc)
                    finish(t, c, x, value, left_over)

        rows(low, high, 2, body)

    def smooth(field):
        def finish(t, c, x, value, left_over):
            field[t, c, x + FO] = value + inv[t, c, x + FO] * left_over

        return finish

    rows(-4, LX + 4, 4, fine_fields)
    diagonals(-2, LX + 2, 1.0, 1.0, 1, FO, a, av, fine_visc, d, inv)
    for made in x_a:
        made.wait_send()
    fine_step(u, -2, LX + 2, smooth(u))
    fine_step(u, -1, LX + 1, smooth(u))

    spread(u, 0, LX, 1.0, 1, FO, a, av)

    def restrict(X):
        for c in range(3):
            total = None
            for k in range(2):
                r = 2 * X + k + FO
                value = u[0, c, r]
                ub[0, c, r] = value
                part = coupled(0, c, r, 1.0, a[0, r], cf[0, 2 * X + k + CO])
                part = f[0, c, r] - d[0, c, r] * value + part
                total = part if total is None else total + part
            other = jnp.where(lanes() % 2 == 0, pltpu.roll(total, 127, 1), pltpu.roll(total, 1, 1))
            kr[0, c, X + KO] = total + other

    rows(0, LX // 2, 1, restrict)

    x_b = to_both_rows(tri(ub), FO, 3, LX)
    x_b += to_both_rows(tri(kr), KO, 5, LX // 2)

    def pack_b(ref, offset):
        def do(x, slot):
            pb[slot] = pack([ref[0, c, x + offset] for c in range(3)])

        return do

    def unpack_b(ref, offset):
        def do(x, slot):
            got = unpack(pbl[slot], pbr[slot], 3)
            for c in range(3):
                ref[1, c, x + offset] = got[c]

        return do

    def own_b(do_u, do_k):
        def body(X):
            do_u(2 * X, 2 * X)
            do_u(2 * X + 1, 2 * X + 1)
            do_k(X, LX + X)

        rows(0, LX // 2, 2, body)

    def halo_b(do_u, do_k):
        for j in range(3):
            do_u(j - 3, 24 + j)
            do_u(LX + j, 27 + j)
        for j in range(5):
            do_k(j - 5, 30 + j)
            do_k(LX // 2 + j, 35 + j)

    own_b(pack_b(ub, FO), pack_b(kr, KO))
    y_own_b = to_both_lanes(pb, pbl, pbr, 0, PACK_B_OWN)
    rows(-6, LX // 2 + 6, 4, coarse_fields)
    for made in x_b:
        made.wait_recv()
    halo_b(pack_b(ub, FO), pack_b(kr, KO))
    y_halo_b = to_both_lanes(pb, pbl, pbr, PACK_B_OWN, PACK_B - PACK_B_OWN)
    diagonals(-5, LX // 2 + 5, 0.5, 4.0, 2, KO, ka, kav, coarse_visc, kd, kinv)
    for made in y_own_b:
        made.wait_recv()
    own_b(unpack_b(ub, FO), unpack_b(kr, KO))
    for made in y_halo_b:
        made.wait_recv()
    halo_b(unpack_b(ub, FO), unpack_b(kr, KO))

    def first_coarse(x):
        for t in range(2):
            for c in range(3):
                kc[t, c, x + KO] = kinv[t, c, x + KO] * kr[t, c, x + KO]

    def coarse_step(low, high):
        spread(kc, low, high, 0.5, 2, KO, ka, kav)

        def body(x):
            r = x + KO
            for t in range(2):
                flag, visc = ka[t, r], kv[t, r]
                for c in range(3):
                    value = kc[t, c, r]
                    left_over = kr[t, c, r] - kd[t, c, r] * value
                    left_over = left_over + coupled(t, c, r, 0.5, flag, visc)
                    kc[t, c, r] = value + kinv[t, c, r] * left_over

        rows(low, high, 2, body)

    half = LX // 2
    rows(-5, half + 5, 3, first_coarse)
    coarse_step(-4, half + 4)
    coarse_step(-3, half + 3)
    coarse_step(-2, half + 2)

    def correct(X):
        for t in range(2):
            for c in range(3):
                step = kc[t, c, X + KO]
                for k in range(2):
                    ub[t, c, 2 * X + k + FO] = ub[t, c, 2 * X + k + FO] + step

    def correct_row(x, X):
        for t in range(2):
            for c in range(3):
                ub[t, c, x + FO] = ub[t, c, x + FO] + kc[t, c, X + KO]

    for made in x_b:
        made.wait_send()
    rows(-1, half + 1, 2, correct)
    correct_row(-3, -2)
    correct_row(LX + 2, half + 1)
    fine_step(ub, -2, LX + 2, smooth(ub))
    fine_step(ub, -1, LX + 1, smooth(ub))

    def finish(t, c, x, value, left_over):
        out_u[c, x] = value
        out_r[c, x] = left_over

    fine_step(ub, 0, LX, finish, (0,))

    for made in y_own + y_halo + y_own_b + y_halo_b:
        made.wait_send()


def shards(ntx, nty, forcing, start_state, ice_mask, class_ids, eta_table, friction):
    vmem = pl.BlockSpec(memory_space=pltpu.VMEM)

    def tiles(*lead):
        return pltpu.VMEM(lead + (8, 128), jnp.float32)

    out = jax.ShapeDtypeStruct((3, LX, 8, 128), jnp.float32)
    fine, coarse = tiles(2, 3, FROWS), tiles(2, 3, KROWS)
    adjoint, residual = pl.pallas_call(
        functools.partial(kernel, ntx, nty),
        out_shape=(out, out),
        in_specs=[pl.BlockSpec(memory_space=pltpu.SMEM)] + [vmem] * 5,
        out_specs=(vmem, vmem),
        scratch_shapes=[
            fine, fine, tiles(2, CROWS), tiles(2, FROWS), tiles(2, FROWS), fine, fine, fine,
            tiles(2, 2, 3, FROWS), tiles(2, KROWS), tiles(2, KROWS), tiles(2, KROWS),
            coarse, coarse, coarse, coarse,
            tiles(PACK_A), tiles(PACK_A), tiles(PACK_A),
            tiles(PACK_B), tiles(PACK_B), tiles(PACK_B),
            pltpu.SemaphoreType.DMA((18,)), pltpu.SemaphoreType.DMA((18,)),
        ],
        compiler_params=pltpu.CompilerParams(
            collective_id=0, has_side_effects=True, vmem_limit_bytes=32 * 1024 * 1024
        ),
    )(eta_table, forcing, start_state, ice_mask, class_ids, friction)

    def back(values):
        return jnp.transpose(values[:, :, :NZ], (0, 2, 1, 3))

    return back(adjoint), back(residual)


def solution(mesh):
    return jax.shard_map(
        functools.partial(shards, mesh.shape["tx"], mesh.shape["ty"]),
        mesh=mesh,
        in_specs=(
            P(None, None, "tx", "ty"),
            P(None, None, "tx", "ty"),
            P("tx", "ty"),
            P(None, "tx", "ty"),
            P(),
            P("tx", "ty"),
        ),
        out_specs=(P(None, None, "tx", "ty"), P(None, None, "tx", "ty")),
        check_vma=False,
    )
```

```python
import functools

import jax
import jax.numpy as jnp
from jax import lax
from jax.experimental import pallas as pl
from jax.experimental.pallas import tpu as pltpu
from jax.sharding import PartitionSpec as P

DAMPING = 0.6
REACTION = 0.05
NZ = 6
LX = 16
FO = 4
CO = 12
KO = 6
FROWS = LX + 2 * FO
CROWS = LX + 2 * CO
KROWS = LX // 2 + 2 * KO
PACK_A_OWN, PACK_A = 32, 48
PACK_B_OWN, PACK_B = 24, 40


def lanes():
    return lax.broadcasted_iota(jnp.int32, (8, 128), 1)


def layers():
    return lax.broadcasted_iota(jnp.int32, (8, 128), 0)


def rows(low, high, body):
    step = next(k for k in (4, 3, 2) if (high - low) % k == 0)

    def run(i, carry):
        for k in range(step):
            body(low + i * step + k)
        return carry

    lax.fori_loop(0, (high - low) // step, run, 0)


def along_y(tiles, weights, shift, edges):
    mains, halo = tiles[:3], tiles[3]
    lane = lanes()
    out = []
    for c in range(3):
        near = pltpu.roll(halo, 112 - 32 * c, 1)
        below = pltpu.roll(jnp.where(lane >= 128 - shift, near, mains[c]), shift, 1)
        above = pltpu.roll(jnp.where(lane < shift, near, mains[c]), 128 - shift, 1)
        out.append(mains[c] + weights[c] * (below + above))
    if edges:
        near, place = pack(mains), lane % 32
        below = pltpu.roll(jnp.where((place >= 16 - shift) & (place < 16), near, halo), shift, 1)
        above = pltpu.roll(
            jnp.where((place >= 16) & (place < 16 + shift), near, halo), 128 - shift, 1
        )
        out.append(halo + weights[3] * (below + above))
    return out


def factors(base, doubled):
    each = [base * (2.0 if c == doubled else 1.0) for c in range(3)]
    packed = jnp.where(lanes() // 32 == doubled, 2.0 * base, base).astype(jnp.float32)
    return each + [packed]


def along_z(tile, weight):
    return tile + weight * (pltpu.roll(tile, 1, 0) + pltpu.roll(tile, 7, 0))


def pack(items):
    packed = pltpu.roll(items[0], 16, 1)
    for j in range(1, len(items)):
        packed = jnp.where(lanes() >= 32 * j, pltpu.roll(items[j], 16 + 32 * j, 1), packed)
    return packed


def edges_of(from_left, from_right):
    return jnp.where(lanes() % 32 < 16, from_left, from_right)


def repeated(packed, j):
    out = packed if j == 0 else pltpu.roll(packed, 128 - 32 * j, 1)
    for c in (1, 2):
        moved = pltpu.roll(packed, (32 * (c - j)) % 128, 1) if c != j else packed
        out = jnp.where(lanes() >= 32 * c, moved, out)
    return out


def kernel(
    ntx, nty,
    eta, forcing, start, mask, classes, friction, out_u, out_r,
    u, f, cf, a, av, d, inv, ub, g, ka, kav, kv, kd, kinv, kr, kc,
    pa, pal, par, pb, pbl, pbr, in_start, in_forcing, in_classes, in_mask, in_friction, send, recv, load,
):
    tx, ty = lax.axis_index("tx"), lax.axis_index("ty")
    up, down = lax.rem(tx + 1, ntx), lax.rem(tx + ntx - 1, ntx)
    right, left = lax.rem(ty + 1, nty), lax.rem(ty + nty - 1, nty)
    pairs = ((classes, in_classes), (mask, in_mask), (friction, in_friction),
             (start, in_start), (forcing, in_forcing))
    loads = [pltpu.make_async_copy(src, dst, load.at[k]) for k, (src, dst) in enumerate(pairs)]
    for made in loads:
        made.start()
    barrier = pltpu.get_barrier_semaphore()
    for where in ({"tx": up}, {"tx": down}, {"ty": right}, {"ty": left}):
        pl.semaphore_signal(barrier, inc=1, device_id=where, device_id_type=pl.DeviceIdType.MESH)

    zero = jnp.zeros((LX, 128), jnp.float32)
    for c in range(3):
        for z in range(NZ, 8):
            u[c, FO : FO + LX, z, :] = zero
            f[c, FO : FO + LX, z, :] = zero
    for made in loads[:3]:
        made.wait()
    for z in range(NZ):
        ids = in_classes[z]
        visc = jnp.zeros((LX, 128), jnp.float32)
        for k in range(eta.shape[0]):
            visc = jnp.where(ids == k, eta[k], visc)
        cf[0, CO : CO + LX, z, :] = visc
    kind = in_mask[...]
    cf[0, CO : CO + LX, 6, :] = jnp.where(kind != 0, 1.0, 0.0).astype(jnp.float32)
    cf[0, CO : CO + LX, 7, :] = jnp.where(kind == 1, in_friction[...], 0.0)

    used = [0]

    def copy(src, dst, where):
        k = used[0]
        used[0] += 1
        made = pltpu.make_async_remote_copy(
            src_ref=src, dst_ref=dst, send_sem=send.at[k], recv_sem=recv.at[k],
            device_id=where, device_id_type=pl.DeviceIdType.MESH,
        )
        made.start()
        return made

    def to_both_rows(make, first, count, own):
        top = copy(make(first + own - count, count), make(first - count, count), {"tx": up})
        low = copy(make(first, count), make(first + own, count), {"tx": down})
        return [top, low]

    def to_both_lanes(packed, from_left, from_right, first, count):
        part = pl.ds(first, count)
        return [
            copy(packed.at[part], from_left.at[part], {"ty": right}),
            copy(packed.at[part], from_right.at[part], {"ty": left}),
        ]

    def tri(ref):
        return lambda first, count: ref.at[pl.ds(0, 3), pl.ds(first, count)]

    pl.semaphore_wait(barrier, 4)
    x_a = to_both_rows(lambda first, count: cf.at[0, pl.ds(first, count)], CO, 12, LX)
    for made, ref, src in ((loads[3], u, in_start), (loads[4], f, in_forcing)):
        made.wait()
        for c in range(3):
            for z in range(NZ):
                ref[c, FO : FO + LX, z, :] = src[c, z]
        x_a += to_both_rows(tri(ref), FO, 4 if ref is u else 2, LX)

    def pack_u(x, slot):
        pa[slot] = pack([u[c, x + FO] for c in range(3)] + [cf[0, x + CO]])

    def pack_f(x, slot):
        pa[slot] = pack([f[c, x + FO] for c in range(3)])

    def pack_k(x, slot):
        pa[slot] = pack([cf[0, x + CO + j] for j in range(4)])

    def unpack_u(x, slot):
        both = edges_of(pal[slot], par[slot])
        u[3, x + FO] = both
        cf[1, x + CO] = repeated(both, 3)

    def unpack_f(x, slot):
        f[3, x + FO] = edges_of(pal[slot], par[slot])

    def unpack_k(x, slot):
        both = edges_of(pal[slot], par[slot])
        for j in range(4):
            cf[1, x + CO + j] = repeated(both, j)

    def own_a(do_u, do_f):
        def body(x):
            do_u(x, x)
            do_f(x, x + LX)

        rows(0, LX, body)

    def halo_a(do_u, do_f, do_k):
        for j in range(4):
            do_u(j - 4, 32 + j)
            do_u(LX + j, 36 + j)
        for j in range(2):
            do_f(j - 2, 40 + j)
            do_f(LX + j, 42 + j)
            do_k(4 * j - 12, 44 + j)
            do_k(LX + 4 + 4 * j, 46 + j)

    own_a(pack_u, pack_f)
    y_own = to_both_lanes(pa, pal, par, 0, PACK_A_OWN)
    for made in x_a:
        made.wait_recv()
    halo_a(pack_u, pack_f, pack_k)
    y_halo = to_both_lanes(pa, pal, par, PACK_A_OWN, PACK_A - PACK_A_OWN)
    for made in y_own:
        made.wait_recv()
    own_a(unpack_u, unpack_f)
    for made in y_halo:
        made.wait_recv()
    halo_a(unpack_u, unpack_f, unpack_k)

    in_column = layers() < NZ
    beyond = ((lanes() % 32 >= 16) & (ty == nty - 1)) | ((lanes() % 32 < 16) & (ty == 0))
    inside = (in_column, in_column & jnp.logical_not(beyond))

    def row_inside(x, count):
        return jnp.logical_not(((x < 0) & (tx == 0)) | ((x >= count) & (tx == ntx - 1)))

    def fine_fields(x):
        for t in range(2):
            tile = cf[t, x + CO]
            keep = inside[t] & row_inside(x, LX)
            active = jnp.where(keep, jnp.broadcast_to(tile[6:7], (8, 128)), 0.0)
            a[t, x + FO] = active
            av[t, x + FO] = active * tile

    def coarse_fields(x):
        for t in range(2):
            tile = cf[t, 2 * x + CO] + cf[t, 2 * x + 1 + CO]
            other = jnp.where(lanes() % 2 == 0, pltpu.roll(tile, 127, 1), pltpu.roll(tile, 1, 1))
            tile = tile + other
            keep = inside[t] & row_inside(x, LX // 2)
            active = jnp.where(keep, 0.25 * jnp.broadcast_to(tile[6:7], (8, 128)), 0.0)
            kv[t, x + KO] = tile
            ka[t, x + KO] = active
            kav[t, x + KO] = active * tile

    def spread(field, low, high, spacing, shift, offset, flags, products, edges=True):
        weights_y, weights_z = factors(0.25 * spacing, 1), factors(0.5, 2)

        def body(x):
            r = x + offset
            for k, scale in enumerate((flags, products)):
                own, beside = scale[0, r], scale[1, r]
                tiles = [own] * 3 + [beside]
                if field is not None:
                    tiles = [tiles[c] * field[c, r] for c in range(4)]
                for c, tile in enumerate(along_y(tiles, weights_y, shift, edges)):
                    g[k, c, r] = along_z(tile, weights_z[c])

        rows(low - 1, high + 1, body)

    def coupled(c, r, weights_x, flag, visc):
        p = g[0, c, r] + weights_x[c] * (g[0, c, r - 1] + g[0, c, r + 1])
        q = g[1, c, r] + weights_x[c] * (g[1, c, r - 1] + g[1, c, r + 1])
        return 2.0 * flag * (visc * p + q)

    def diagonals(low, high, spacing, ocean, shift, offset, flags, products, visc, diag, scaled):
        spread(None, low, high, spacing, shift, offset, flags, products)
        weights_x = factors(0.25 * spacing, 0)

        def body(x):
            r = x + offset
            for t in range(2):
                tile, flag, product = visc(t, x), flags[t, r], products[t, r]
                bottom = layers() == 0
                if t == 1:
                    bottom = bottom & (lanes() < 64)
                basal = jnp.where(bottom, jnp.broadcast_to(tile[7:8], (8, 128)), 0.0)
                base = REACTION * product + ocean * (1.0 - flag)
                for c in (3,) if t == 1 else range(3):
                    whole = coupled(c, r, weights_x, flag, tile) + base
                    if c != 2:
                        whole = whole + basal
                    diag[c, r] = whole
                    scaled[c, r] = DAMPING / (whole - 4.0 * flag * product)

        rows(low, high, body)

    def fine_visc(t, x):
        return cf[t, x + CO]

    def coarse_visc(t, x):
        return kv[t, x + KO]

    def fine_step(field, low, high, finish, edges=True):
        spread(field, low, high, 1.0, 1, FO, a, av, edges)
        weights_x = factors(0.25, 0)

        def body(x):
            r = x + FO
            for c in range(4 if edges else 3):
                flag, visc = a[c // 3, r], cf[c // 3, x + CO]
                value = field[c, r]
                left_over = f[c, r] - d[c, r] * value + coupled(c, r, weights_x, flag, visc)
                finish(c, x, value, left_over)

        rows(low, high, body)

    def smooth(field):
        def finish(c, x, value, left_over):
            field[c, x + FO] = value + inv[c, x + FO] * left_over

        return finish

    rows(-4, LX + 4, fine_fields)
    diagonals(-2, LX + 2, 1.0, 1.0, 1, FO, a, av, fine_visc, d, inv)
    for made in x_a:
        made.wait_send()
    fine_step(u, -2, LX + 2, smooth(u))
    fine_step(u, -1, LX + 1, smooth(u))

    spread(u, 0, LX, 1.0, 1, FO, a, av, False)
    fine_x = factors(0.25, 0)

    def restrict(X):
        for c in range(3):
            total = None
            for k in range(2):
                r = 2 * X + k + FO
                value = u[c, r]
                ub[c, r] = value
                part = coupled(c, r, fine_x, a[0, r], cf[0, 2 * X + k + CO])
                part = f[c, r] - d[c, r] * value + part
                total = part if total is None else total + part
            other = jnp.where(lanes() % 2 == 0, pltpu.roll(total, 127, 1), pltpu.roll(total, 1, 1))
            kr[c, X + KO] = total + other

    rows(0, LX // 2, restrict)

    x_b = to_both_rows(tri(ub), FO, 3, LX)
    x_b += to_both_rows(tri(kr), KO, 5, LX // 2)

    def pack_b(ref, offset):
        def do(x, slot):
            pb[slot] = pack([ref[c, x + offset] for c in range(3)])

        return do

    def unpack_b(ref, offset):
        def do(x, slot):
            ref[3, x + offset] = edges_of(pbl[slot], pbr[slot])

        return do

    def own_b(do_u, do_k):
        def body(X):
            do_u(2 * X, 2 * X)
            do_u(2 * X + 1, 2 * X + 1)
            do_k(X, LX + X)

        rows(0, LX // 2, body)

    def halo_b(do_u, do_k):
        for j in range(3):
            do_u(j - 3, 24 + j)
            do_u(LX + j, 27 + j)
        for j in range(5):
            do_k(j - 5, 30 + j)
            do_k(LX // 2 + j, 35 + j)

    own_b(pack_b(ub, FO), pack_b(kr, KO))
    y_own_b = to_both_lanes(pb, pbl, pbr, 0, PACK_B_OWN)
    rows(-6, LX // 2 + 6, coarse_fields)
    for made in x_b:
        made.wait_recv()
    halo_b(pack_b(ub, FO), pack_b(kr, KO))
    y_halo_b = to_both_lanes(pb, pbl, pbr, PACK_B_OWN, PACK_B - PACK_B_OWN)
    diagonals(-5, LX // 2 + 5, 0.5, 4.0, 2, KO, ka, kav, coarse_visc, kd, kinv)
    for made in y_own_b:
        made.wait_recv()
    own_b(unpack_b(ub, FO), unpack_b(kr, KO))
    for made in y_halo_b:
        made.wait_recv()
    halo_b(unpack_b(ub, FO), unpack_b(kr, KO))

    def first_coarse(x):
        for c in range(4):
            kc[c, x + KO] = kinv[c, x + KO] * kr[c, x + KO]

    def coarse_step(low, high):
        spread(kc, low, high, 0.5, 2, KO, ka, kav)
        weights_x = factors(0.125, 0)

        def body(x):
            r = x + KO
            for c in range(4):
                flag, visc = ka[c // 3, r], kv[c // 3, r]
                value = kc[c, r]
                left_over = kr[c, r] - kd[c, r] * value
                left_over = left_over + coupled(c, r, weights_x, flag, visc)
                kc[c, r] = value + kinv[c, r] * left_over

        rows(low, high, body)

    half = LX // 2
    rows(-5, half + 5, first_coarse)
    coarse_step(-4, half + 4)
    coarse_step(-3, half + 3)
    coarse_step(-2, half + 2)

    def correct_row(x, X):
        for c in range(4):
            ub[c, x + FO] = ub[c, x + FO] + kc[c, X + KO]

    def correct(X):
        correct_row(2 * X, X)
        correct_row(2 * X + 1, X)

    for made in x_b:
        made.wait_send()
    rows(-1, half + 1, correct)
    correct_row(-3, -2)
    correct_row(LX + 2, half + 1)
    fine_step(ub, -2, LX + 2, smooth(ub))
    fine_step(ub, -1, LX + 1, smooth(ub))

    def finish(c, x, value, left_over):
        out_u[c, x] = value
        out_r[c, x] = left_over

    fine_step(ub, 0, LX, finish, False)

    for made in y_own + y_halo + y_own_b + y_halo_b:
        made.wait_send()


def shards(ntx, nty, forcing, start_state, ice_mask, class_ids, eta_table, friction):
    vmem = pl.BlockSpec(memory_space=pltpu.VMEM)

    def tiles(*lead):
        return pltpu.VMEM(lead + (8, 128), jnp.float32)

    out = jax.ShapeDtypeStruct((3, LX, 8, 128), jnp.float32)
    fine, coarse = tiles(4, FROWS), tiles(4, KROWS)
    hbm = pl.BlockSpec(memory_space=pltpu.HBM)
    adjoint, residual = pl.pallas_call(
        functools.partial(kernel, ntx, nty),
        out_shape=(out, out),
        in_specs=[pl.BlockSpec(memory_space=pltpu.SMEM)] + [hbm] * 5,
        out_specs=(vmem, vmem),
        scratch_shapes=[
            fine, fine, tiles(2, CROWS), tiles(2, FROWS), tiles(2, FROWS), fine, fine, fine,
            tiles(2, 4, FROWS), tiles(2, KROWS), tiles(2, KROWS), tiles(2, KROWS),
            coarse, coarse, coarse, coarse,
            tiles(PACK_A), tiles(PACK_A), tiles(PACK_A),
            tiles(PACK_B), tiles(PACK_B), tiles(PACK_B),
            pltpu.VMEM((3, NZ, LX, 128), jnp.float32), pltpu.VMEM((3, NZ, LX, 128), jnp.float32),
            pltpu.VMEM((NZ, LX, 128), jnp.int32), pltpu.VMEM((LX, 128), jnp.int32),
            pltpu.VMEM((LX, 128), jnp.float32),
            pltpu.SemaphoreType.DMA((18,)), pltpu.SemaphoreType.DMA((18,)), pltpu.SemaphoreType.DMA((5,)),
        ],
        compiler_params=pltpu.CompilerParams(
            collective_id=0, has_side_effects=True, vmem_limit_bytes=32 * 1024 * 1024
        ),
    )(eta_table, forcing, start_state, ice_mask, class_ids, friction)

    def back(values):
        return jnp.transpose(values[:, :, :NZ], (0, 2, 1, 3))

    return back(adjoint), back(residual)


def solution(mesh):
    return jax.shard_map(
        functools.partial(shards, mesh.shape["tx"], mesh.shape["ty"]),
        mesh=mesh,
        in_specs=(
            P(None, None, "tx", "ty"),
            P(None, None, "tx", "ty"),
            P("tx", "ty"),
            P(None, "tx", "ty"),
            P(),
            P("tx", "ty"),
        ),
        out_specs=(P(None, None, "tx", "ty"), P(None, None, "tx", "ty")),
        check_vma=False,
    )
```

```python
import functools

import jax
import jax.numpy as jnp
from jax import lax
from jax.experimental import pallas as pl
from jax.experimental.pallas import tpu as pltpu
from jax.sharding import PartitionSpec as P

DAMPING = 0.6
REACTION = 0.05
NZ = 6
LX = 16
FO = 4
CO = 12
KO = 6
FROWS = LX + 2 * FO
CROWS = LX + 2 * CO
KROWS = LX // 2 + 2 * KO
PACK_A_OWN, PACK_A = 32, 48
PACK_B_OWN, PACK_B = 24, 40


def lanes():
    return lax.broadcasted_iota(jnp.int32, (8, 128), 1)


def layers():
    return lax.broadcasted_iota(jnp.int32, (8, 128), 0)


def rows(low, high, body):
    step = next(k for k in (4, 3, 2) if (high - low) % k == 0)

    def run(i, carry):
        for k in range(step):
            body(low + i * step + k)
        return carry

    lax.fori_loop(0, (high - low) // step, run, 0)


def along_y(tiles, weights, shift, edges):
    mains, halo = tiles[:3], tiles[3]
    lane = lanes()
    out = []
    for c in range(3):
        near = pltpu.roll(halo, 112 - 32 * c, 1)
        below = pltpu.roll(jnp.where(lane >= 128 - shift, near, mains[c]), shift, 1)
        above = pltpu.roll(jnp.where(lane < shift, near, mains[c]), 128 - shift, 1)
        out.append(mains[c] + weights[c] * (below + above))
    if edges:
        near, place = pack(mains), lane % 32
        below = pltpu.roll(jnp.where((place >= 16 - shift) & (place < 16), near, halo), shift, 1)
        above = pltpu.roll(
            jnp.where((place >= 16) & (place < 16 + shift), near, halo), 128 - shift, 1
        )
        out.append(halo + weights[3] * (below + above))
    return out


def factors(base, doubled):
    each = [base * (2.0 if c == doubled else 1.0) for c in range(3)]
    packed = jnp.where(lanes() // 32 == doubled, 2.0 * base, base).astype(jnp.float32)
    return each + [packed]


def along_z(tile, weight):
    return tile + weight * (pltpu.roll(tile, 1, 0) + pltpu.roll(tile, 7, 0))


def pack(items):
    packed = pltpu.roll(items[0], 16, 1)
    for j in range(1, len(items)):
        packed = jnp.where(lanes() >= 32 * j, pltpu.roll(items[j], 16 + 32 * j, 1), packed)
    return packed


def edges_of(from_left, from_right):
    return jnp.where(lanes() % 32 < 16, from_left, from_right)


def repeated(packed, j):
    out = packed if j == 0 else pltpu.roll(packed, 128 - 32 * j, 1)
    for c in (1, 2):
        moved = pltpu.roll(packed, (32 * (c - j)) % 128, 1) if c != j else packed
        out = jnp.where(lanes() >= 32 * c, moved, out)
    return out


def kernel(
    ntx, nty,
    table, forcing, start, mask, classes, friction, out_u, out_r,
    u, f, cf, a, av, d, inv, ub, g, ka, kav, kv, kd, kinv, kr, kc,
    pa, pal, par, pb, pbl, pbr, in_start, in_forcing, in_classes, in_mask, in_friction, eta, send, recv, load,
):
    tx, ty = lax.axis_index("tx"), lax.axis_index("ty")
    up, down = lax.rem(tx + 1, ntx), lax.rem(tx + ntx - 1, ntx)
    right, left = lax.rem(ty + 1, nty), lax.rem(ty + nty - 1, nty)
    pairs = ((classes, in_classes), (mask, in_mask), (friction, in_friction),
             (table, eta), (start, in_start), (forcing, in_forcing))
    loads = [pltpu.make_async_copy(src, dst, load.at[k]) for k, (src, dst) in enumerate(pairs)]
    for made in loads:
        made.start()
    barrier = pltpu.get_barrier_semaphore()
    for where in ({"tx": up}, {"tx": down}, {"ty": right}, {"ty": left}):
        pl.semaphore_signal(barrier, inc=1, device_id=where, device_id_type=pl.DeviceIdType.MESH)

    zero = jnp.zeros((LX, 128), jnp.float32)
    for c in range(3):
        for z in range(NZ, 8):
            u[c, FO : FO + LX, z, :] = zero
            f[c, FO : FO + LX, z, :] = zero
    for made in loads[:4]:
        made.wait()
    for z in range(NZ):
        ids = in_classes[z]
        visc = jnp.zeros((LX, 128), jnp.float32)
        for k in range(eta.shape[0]):
            visc = jnp.where(ids == k, eta[k], visc)
        cf[0, CO : CO + LX, z, :] = visc
    kind = in_mask[...]
    cf[0, CO : CO + LX, 6, :] = jnp.where(kind != 0, 1.0, 0.0).astype(jnp.float32)
    cf[0, CO : CO + LX, 7, :] = jnp.where(kind == 1, in_friction[...], 0.0)

    used = [0]

    def copy(src, dst, where):
        k = used[0]
        used[0] += 1
        made = pltpu.make_async_remote_copy(
            src_ref=src, dst_ref=dst, send_sem=send.at[k], recv_sem=recv.at[k],
            device_id=where, device_id_type=pl.DeviceIdType.MESH,
        )
        made.start()
        return made

    def to_both_rows(make, first, count, own):
        top = copy(make(first + own - count, count), make(first - count, count), {"tx": up})
        low = copy(make(first, count), make(first + own, count), {"tx": down})
        return [top, low]

    def to_both_lanes(packed, from_left, from_right, first, count):
        part = pl.ds(first, count)
        return [
            copy(packed.at[part], from_left.at[part], {"ty": right}),
            copy(packed.at[part], from_right.at[part], {"ty": left}),
        ]

    def tri(ref):
        return lambda first, count: ref.at[pl.ds(0, 3), pl.ds(first, count)]

    pl.semaphore_wait(barrier, 4)
    x_a = to_both_rows(lambda first, count: cf.at[0, pl.ds(first, count)], CO, 12, LX)
    for made, ref, src in ((loads[4], u, in_start), (loads[5], f, in_forcing)):
        made.wait()
        for c in range(3):
            for z in range(NZ):
                ref[c, FO : FO + LX, z, :] = src[c, z]
        x_a += to_both_rows(tri(ref), FO, 4 if ref is u else 2, LX)

    def pack_u(x, slot):
        pa[slot] = pack([u[c, x + FO] for c in range(3)] + [cf[0, x + CO]])

    def pack_f(x, slot):
        pa[slot] = pack([f[c, x + FO] for c in range(3)])

    def pack_k(x, slot):
        pa[slot] = pack([cf[0, x + CO + j] for j in range(4)])

    def unpack_u(x, slot):
        both = edges_of(pal[slot], par[slot])
        u[3, x + FO] = both
        cf[1, x + CO] = repeated(both, 3)

    def unpack_f(x, slot):
        f[3, x + FO] = edges_of(pal[slot], par[slot])

    def unpack_k(x, slot):
        both = edges_of(pal[slot], par[slot])
        for j in range(4):
            cf[1, x + CO + j] = repeated(both, j)

    def own_a(do_u, do_f):
        def body(x):
            do_u(x, x)
            do_f(x, x + LX)

        rows(0, LX, body)

    def halo_a(do_u, do_f, do_k):
        for j in range(4):
            do_u(j - 4, 32 + j)
            do_u(LX + j, 36 + j)
        for j in range(2):
            do_f(j - 2, 40 + j)
            do_f(LX + j, 42 + j)
            do_k(4 * j - 12, 44 + j)
            do_k(LX + 4 + 4 * j, 46 + j)

    own_a(pack_u, pack_f)
    y_own = to_both_lanes(pa, pal, par, 0, PACK_A_OWN)
    for made in x_a:
        made.wait_recv()
    halo_a(pack_u, pack_f, pack_k)
    y_halo = to_both_lanes(pa, pal, par, PACK_A_OWN, PACK_A - PACK_A_OWN)
    for made in y_own:
        made.wait_recv()
    own_a(unpack_u, unpack_f)
    for made in y_halo:
        made.wait_recv()
    halo_a(unpack_u, unpack_f, unpack_k)

    in_column = layers() < NZ
    beyond = ((lanes() % 32 >= 16) & (ty == nty - 1)) | ((lanes() % 32 < 16) & (ty == 0))
    inside = (in_column, in_column & jnp.logical_not(beyond))

    def row_inside(x, count):
        return jnp.logical_not(((x < 0) & (tx == 0)) | ((x >= count) & (tx == ntx - 1)))

    def fine_fields(x):
        for t in range(2):
            tile = cf[t, x + CO]
            keep = inside[t] & row_inside(x, LX)
            active = jnp.where(keep, jnp.broadcast_to(tile[6:7], (8, 128)), 0.0)
            a[t, x + FO] = active
            av[t, x + FO] = active * tile

    def coarse_fields(x):
        for t in range(2):
            tile = cf[t, 2 * x + CO] + cf[t, 2 * x + 1 + CO]
            other = jnp.where(lanes() % 2 == 0, pltpu.roll(tile, 127, 1), pltpu.roll(tile, 1, 1))
            tile = tile + other
            keep = inside[t] & row_inside(x, LX // 2)
            active = jnp.where(keep, 0.25 * jnp.broadcast_to(tile[6:7], (8, 128)), 0.0)
            kv[t, x + KO] = tile
            ka[t, x + KO] = active
            kav[t, x + KO] = active * tile

    def spread(field, low, high, spacing, shift, offset, flags, products, edges=True):
        weights_y, weights_z = factors(0.25 * spacing, 1), factors(0.5, 2)

        def body(x):
            r = x + offset
            for k, scale in enumerate((flags, products)):
                own, beside = scale[0, r], scale[1, r]
                tiles = [own] * 3 + [beside]
                if field is not None:
                    tiles = [tiles[c] * field[c, r] for c in range(4)]
                for c, tile in enumerate(along_y(tiles, weights_y, shift, edges)):
                    g[k, c, r] = along_z(tile, weights_z[c])

        rows(low - 1, high + 1, body)

    def coupled(c, r, weights_x, flag, visc):
        p = g[0, c, r] + weights_x[c] * (g[0, c, r - 1] + g[0, c, r + 1])
        q = g[1, c, r] + weights_x[c] * (g[1, c, r - 1] + g[1, c, r + 1])
        return 2.0 * flag * (visc * p + q)

    def diagonals(low, high, spacing, ocean, shift, offset, flags, products, visc, diag, scaled):
        spread(None, low, high, spacing, shift, offset, flags, products)
        weights_x = factors(0.25 * spacing, 0)

        def body(x):
            r = x + offset
            for t in range(2):
                tile, flag, product = visc(t, x), flags[t, r], products[t, r]
                bottom = layers() == 0
                if t == 1:
                    bottom = bottom & (lanes() < 64)
                basal = jnp.where(bottom, jnp.broadcast_to(tile[7:8], (8, 128)), 0.0)
                base = REACTION * product + ocean * (1.0 - flag)
                for c in (3,) if t == 1 else range(3):
                    whole = coupled(c, r, weights_x, flag, tile) + base
                    if c != 2:
                        whole = whole + basal
                    diag[c, r] = whole
                    scaled[c, r] = DAMPING / (whole - 4.0 * flag * product)

        rows(low, high, body)

    def fine_visc(t, x):
        return cf[t, x + CO]

    def coarse_visc(t, x):
        return kv[t, x + KO]

    def fine_step(field, low, high, finish, edges=True):
        spread(field, low, high, 1.0, 1, FO, a, av, edges)
        weights_x = factors(0.25, 0)

        def body(x):
            r = x + FO
            for c in range(4 if edges else 3):
                flag, visc = a[c // 3, r], cf[c // 3, x + CO]
                value = field[c, r]
                left_over = f[c, r] - d[c, r] * value + coupled(c, r, weights_x, flag, visc)
                finish(c, x, value, left_over)

        rows(low, high, body)

    def smooth(field):
        def finish(c, x, value, left_over):
            field[c, x + FO] = value + inv[c, x + FO] * left_over

        return finish

    rows(-4, LX + 4, fine_fields)
    diagonals(-2, LX + 2, 1.0, 1.0, 1, FO, a, av, fine_visc, d, inv)
    for made in x_a:
        made.wait_send()
    fine_step(u, -2, LX + 2, smooth(u))
    fine_step(u, -1, LX + 1, smooth(u))

    spread(u, 0, LX, 1.0, 1, FO, a, av, False)
    fine_x = factors(0.25, 0)

    def restrict(X):
        for c in range(3):
            total = None
            for k in range(2):
                r = 2 * X + k + FO
                value = u[c, r]
                ub[c, r] = value
                part = coupled(c, r, fine_x, a[0, r], cf[0, 2 * X + k + CO])
                part = f[c, r] - d[c, r] * value + part
                total = part if total is None else total + part
            other = jnp.where(lanes() % 2 == 0, pltpu.roll(total, 127, 1), pltpu.roll(total, 1, 1))
            kr[c, X + KO] = total + other

    rows(0, LX // 2, restrict)

    x_b = to_both_rows(tri(ub), FO, 3, LX)
    x_b += to_both_rows(tri(kr), KO, 5, LX // 2)

    def pack_b(ref, offset):
        def do(x, slot):
            pb[slot] = pack([ref[c, x + offset] for c in range(3)])

        return do

    def unpack_b(ref, offset):
        def do(x, slot):
            ref[3, x + offset] = edges_of(pbl[slot], pbr[slot])

        return do

    def own_b(do_u, do_k):
        def body(X):
            do_u(2 * X, 2 * X)
            do_u(2 * X + 1, 2 * X + 1)
            do_k(X, LX + X)

        rows(0, LX // 2, body)

    def halo_b(do_u, do_k):
        for j in range(3):
            do_u(j - 3, 24 + j)
            do_u(LX + j, 27 + j)
        for j in range(5):
            do_k(j - 5, 30 + j)
            do_k(LX // 2 + j, 35 + j)

    own_b(pack_b(ub, FO), pack_b(kr, KO))
    y_own_b = to_both_lanes(pb, pbl, pbr, 0, PACK_B_OWN)
    rows(-6, LX // 2 + 6, coarse_fields)
    for made in x_b:
        made.wait_recv()
    halo_b(pack_b(ub, FO), pack_b(kr, KO))
    y_halo_b = to_both_lanes(pb, pbl, pbr, PACK_B_OWN, PACK_B - PACK_B_OWN)
    diagonals(-5, LX // 2 + 5, 0.5, 4.0, 2, KO, ka, kav, coarse_visc, kd, kinv)
    for made in y_own_b:
        made.wait_recv()
    own_b(unpack_b(ub, FO), unpack_b(kr, KO))
    for made in y_halo_b:
        made.wait_recv()
    halo_b(unpack_b(ub, FO), unpack_b(kr, KO))

    def first_coarse(x):
        for c in range(4):
            kc[c, x + KO] = kinv[c, x + KO] * kr[c, x + KO]

    def coarse_step(low, high):
        spread(kc, low, high, 0.5, 2, KO, ka, kav)
        weights_x = factors(0.125, 0)

        def body(x):
            r = x + KO
            for c in range(4):
                flag, visc = ka[c // 3, r], kv[c // 3, r]
                value = kc[c, r]
                left_over = kr[c, r] - kd[c, r] * value
                left_over = left_over + coupled(c, r, weights_x, flag, visc)
                kc[c, r] = value + kinv[c, r] * left_over

        rows(low, high, body)

    half = LX // 2
    rows(-5, half + 5, first_coarse)
    coarse_step(-4, half + 4)
    coarse_step(-3, half + 3)
    coarse_step(-2, half + 2)

    def correct_row(x, X):
        for c in range(4):
            ub[c, x + FO] = ub[c, x + FO] + kc[c, X + KO]

    def correct(X):
        correct_row(2 * X, X)
        correct_row(2 * X + 1, X)

    for made in x_b:
        made.wait_send()
    rows(-1, half + 1, correct)
    correct_row(-3, -2)
    correct_row(LX + 2, half + 1)
    fine_step(ub, -2, LX + 2, smooth(ub))
    fine_step(ub, -1, LX + 1, smooth(ub))

    def finish(c, x, value, left_over):
        out_u[c, x] = value
        out_r[c, x] = left_over

    fine_step(ub, 0, LX, finish, False)

    for made in y_own + y_halo + y_own_b + y_halo_b:
        made.wait_send()


def shards(ntx, nty, forcing, start_state, ice_mask, class_ids, eta_table, friction):
    vmem = pl.BlockSpec(memory_space=pltpu.VMEM)

    def tiles(*lead):
        return pltpu.VMEM(lead + (8, 128), jnp.float32)

    out = jax.ShapeDtypeStruct((3, LX, 8, 128), jnp.float32)
    fine, coarse = tiles(4, FROWS), tiles(4, KROWS)
    hbm = pl.BlockSpec(memory_space=pltpu.HBM)
    adjoint, residual = pl.pallas_call(
        functools.partial(kernel, ntx, nty),
        out_shape=(out, out),
        in_specs=[hbm] * 6,
        out_specs=(vmem, vmem),
        scratch_shapes=[
            fine, fine, tiles(2, CROWS), tiles(2, FROWS), tiles(2, FROWS), fine, fine, fine,
            tiles(2, 4, FROWS), tiles(2, KROWS), tiles(2, KROWS), tiles(2, KROWS),
            coarse, coarse, coarse, coarse,
            tiles(PACK_A), tiles(PACK_A), tiles(PACK_A),
            tiles(PACK_B), tiles(PACK_B), tiles(PACK_B),
            pltpu.VMEM((3, NZ, LX, 128), jnp.float32), pltpu.VMEM((3, NZ, LX, 128), jnp.float32),
            pltpu.VMEM((NZ, LX, 128), jnp.int32), pltpu.VMEM((LX, 128), jnp.int32),
            pltpu.VMEM((LX, 128), jnp.float32), pltpu.SMEM((16,), jnp.float32),
            pltpu.SemaphoreType.DMA((18,)), pltpu.SemaphoreType.DMA((18,)), pltpu.SemaphoreType.DMA((6,)),
        ],
        compiler_params=pltpu.CompilerParams(
            collective_id=0, has_side_effects=True, vmem_limit_bytes=32 << 20
        ),
    )(*(
        pltpu.with_memory_space_constraint(value, pltpu.HBM)
        for value in (eta_table, forcing, start_state, ice_mask, class_ids, friction)
    ))

    def back(values):
        return jnp.transpose(values[:, :, :NZ], (0, 2, 1, 3))

    return back(adjoint), back(residual)


def solution(mesh):
    return jax.shard_map(
        functools.partial(shards, mesh.shape["tx"], mesh.shape["ty"]),
        mesh=mesh,
        in_specs=(
            P(None, None, "tx", "ty"),
            P(None, None, "tx", "ty"),
            P("tx", "ty"),
            P(None, "tx", "ty"),
            P(),
            P("tx", "ty"),
        ),
        out_specs=(P(None, None, "tx", "ty"), P(None, None, "tx", "ty")),
        check_vma=False,
    )
```

```python
import functools

import jax
import jax.numpy as jnp
from jax import lax
from jax.experimental import pallas as pl
from jax.experimental.pallas import tpu as pltpu
from jax.sharding import PartitionSpec as P

DAMPING = 0.6
REACTION = 0.05
NZ = 6
LX = 16
FO = 4
CO = 12
KO = 6
FROWS = LX + 2 * FO
CROWS = LX + 2 * CO
KROWS = LX // 2 + 2 * KO
PACK_A_OWN, PACK_A = 32, 48
PACK_B_OWN, PACK_B = 24, 40


def lanes():
    return lax.broadcasted_iota(jnp.int32, (8, 128), 1)


def layers():
    return lax.broadcasted_iota(jnp.int32, (8, 128), 0)


def rows(low, high, body):
    step = next(k for k in (4, 3, 2) if (high - low) % k == 0)

    def run(i, carry):
        for k in range(step):
            body(low + i * step + k)
        return carry

    lax.fori_loop(0, (high - low) // step, run, 0)


def beside(tiles, shift, edges=True):
    mains, halo = tiles[:3], tiles[3]
    lane = lanes()
    below, above = [], []
    for c in range(3):
        near = pltpu.roll(halo, 112 - 32 * c, 1)
        below.append(pltpu.roll(jnp.where(lane >= 128 - shift, near, mains[c]), shift, 1))
        above.append(pltpu.roll(jnp.where(lane < shift, near, mains[c]), 128 - shift, 1))
    if edges:
        near, place = pack(mains), lane % 32
        low = (place >= 16 - shift) & (place < 16)
        high = (place >= 16) & (place < 16 + shift)
        below.append(pltpu.roll(jnp.where(low, near, halo), shift, 1))
        above.append(pltpu.roll(jnp.where(high, near, halo), 128 - shift, 1))
    return below, above


def factors(base, doubled):
    each = [base * (2.0 if c == doubled else 1.0) for c in range(3)]
    packed = jnp.where(lanes() // 32 == doubled, 2.0 * base, base).astype(jnp.float32)
    return each + [packed]


def along_z(tile, weight):
    return tile + weight * (pltpu.roll(tile, 1, 0) + pltpu.roll(tile, 7, 0))


def pack(items):
    packed = pltpu.roll(items[0], 16, 1)
    for j in range(1, len(items)):
        packed = jnp.where(lanes() >= 32 * j, pltpu.roll(items[j], 16 + 32 * j, 1), packed)
    return packed


def edges_of(from_left, from_right):
    return jnp.where(lanes() % 32 < 16, from_left, from_right)


def repeated(packed, j):
    out = packed if j == 0 else pltpu.roll(packed, 128 - 32 * j, 1)
    for c in (1, 2):
        moved = pltpu.roll(packed, (32 * (c - j)) % 128, 1) if c != j else packed
        out = jnp.where(lanes() >= 32 * c, moved, out)
    return out


def kernel(
    ntx, nty,
    table, forcing, start, mask, classes, friction, out_u, out_r,
    u, f, cf, a, av, d, inv, ub, g, ka, kav, kv, kd, kinv, kr, kc,
    pa, pal, par, pb, pbl, pbr, in_start, in_forcing, in_classes, in_mask, in_friction, eta, send, recv, load,
):
    tx, ty = lax.axis_index("tx"), lax.axis_index("ty")
    up, down = lax.rem(tx + 1, ntx), lax.rem(tx + ntx - 1, ntx)
    right, left = lax.rem(ty + 1, nty), lax.rem(ty + nty - 1, nty)
    pairs = ((classes, in_classes), (mask, in_mask), (friction, in_friction),
             (table, eta), (start, in_start), (forcing, in_forcing))
    loads = [pltpu.make_async_copy(src, dst, load.at[k]) for k, (src, dst) in enumerate(pairs)]
    for made in loads:
        made.start()
    barrier = pltpu.get_barrier_semaphore()
    for where in ({"tx": up}, {"tx": down}, {"ty": right}, {"ty": left}):
        pl.semaphore_signal(barrier, inc=1, device_id=where, device_id_type=pl.DeviceIdType.MESH)

    zero = jnp.zeros((LX, 128), jnp.float32)
    for c in range(3):
        for z in range(NZ, 8):
            u[c, FO : FO + LX, z, :] = zero
            f[c, FO : FO + LX, z, :] = zero
    for made in loads[:4]:
        made.wait()
    for z in range(NZ):
        ids = in_classes[z]
        visc = jnp.zeros((LX, 128), jnp.float32)
        for k in range(eta.shape[0]):
            visc = jnp.where(ids == k, eta[k], visc)
        cf[0, CO : CO + LX, z, :] = visc
    kind = in_mask[...]
    cf[0, CO : CO + LX, 6, :] = jnp.where(kind != 0, 1.0, 0.0).astype(jnp.float32)
    cf[0, CO : CO + LX, 7, :] = jnp.where(kind == 1, in_friction[...], 0.0)

    used = [0]

    def copy(src, dst, where):
        k = used[0]
        used[0] += 1
        made = pltpu.make_async_remote_copy(
            src_ref=src, dst_ref=dst, send_sem=send.at[k], recv_sem=recv.at[k],
            device_id=where, device_id_type=pl.DeviceIdType.MESH,
        )
        made.start()
        return made

    def to_both_rows(make, first, count, own):
        top = copy(make(first + own - count, count), make(first - count, count), {"tx": up})
        low = copy(make(first, count), make(first + own, count), {"tx": down})
        return [top, low]

    def to_both_lanes(packed, from_left, from_right, first, count):
        part = pl.ds(first, count)
        return [
            copy(packed.at[part], from_left.at[part], {"ty": right}),
            copy(packed.at[part], from_right.at[part], {"ty": left}),
        ]

    def tri(ref):
        return lambda first, count: ref.at[pl.ds(0, 3), pl.ds(first, count)]

    pl.semaphore_wait(barrier, 4)
    x_a = to_both_rows(lambda first, count: cf.at[0, pl.ds(first, count)], CO, 12, LX)
    for made, ref, src in ((loads[4], u, in_start), (loads[5], f, in_forcing)):
        made.wait()
        for c in range(3):
            for z in range(NZ):
                ref[c, FO : FO + LX, z, :] = src[c, z]
        x_a += to_both_rows(tri(ref), FO, 4 if ref is u else 2, LX)

    def pack_u(x, slot):
        pa[slot] = pack([u[c, x + FO] for c in range(3)] + [cf[0, x + CO]])

    def pack_f(x, slot):
        pa[slot] = pack([f[c, x + FO] for c in range(3)])

    def pack_k(x, slot):
        pa[slot] = pack([cf[0, x + CO + j] for j in range(4)])

    def unpack_u(x, slot):
        both = edges_of(pal[slot], par[slot])
        u[3, x + FO] = both
        cf[1, x + CO] = repeated(both, 3)

    def unpack_f(x, slot):
        f[3, x + FO] = edges_of(pal[slot], par[slot])

    def unpack_k(x, slot):
        both = edges_of(pal[slot], par[slot])
        for j in range(4):
            cf[1, x + CO + j] = repeated(both, j)

    def own_a(do_u, do_f):
        def body(x):
            do_u(x, x)
            do_f(x, x + LX)

        rows(0, LX, body)

    def halo_a(do_u, do_f, do_k):
        for j in range(4):
            do_u(j - 4, 32 + j)
            do_u(LX + j, 36 + j)
        for j in range(2):
            do_f(j - 2, 40 + j)
            do_f(LX + j, 42 + j)
            do_k(4 * j - 12, 44 + j)
            do_k(LX + 4 + 4 * j, 46 + j)

    own_a(pack_u, pack_f)
    y_own = to_both_lanes(pa, pal, par, 0, PACK_A_OWN)
    for made in x_a:
        made.wait_recv()
    halo_a(pack_u, pack_f, pack_k)
    y_halo = to_both_lanes(pa, pal, par, PACK_A_OWN, PACK_A - PACK_A_OWN)
    for made in y_own:
        made.wait_recv()
    own_a(unpack_u, unpack_f)
    for made in y_halo:
        made.wait_recv()
    halo_a(unpack_u, unpack_f, unpack_k)

    in_column = layers() < NZ
    beyond = ((lanes() % 32 >= 16) & (ty == nty - 1)) | ((lanes() % 32 < 16) & (ty == 0))
    inside = (in_column, in_column & jnp.logical_not(beyond))

    def row_inside(x, count):
        return jnp.logical_not(((x < 0) & (tx == 0)) | ((x >= count) & (tx == ntx - 1)))

    def keep_beside(ref, pair, r, shift):
        below, above = beside([pair[0]] * 3 + [pair[1]], shift)
        for t in range(2):
            ref[0, t, r], ref[1, t, r], ref[2, t, r] = pair[t], below[3 * t], above[3 * t]

    def fine_fields(x):
        pairs_a, pairs_av = [], []
        for t in range(2):
            tile = cf[t, x + CO]
            keep = inside[t] & row_inside(x, LX)
            active = jnp.where(keep, jnp.broadcast_to(tile[6:7], (8, 128)), 0.0)
            pairs_a.append(active)
            pairs_av.append(active * tile)
        keep_beside(a, pairs_a, x + FO, 1)
        keep_beside(av, pairs_av, x + FO, 1)

    def coarse_fields(x):
        pairs_a, pairs_av = [], []
        for t in range(2):
            tile = cf[t, 2 * x + CO] + cf[t, 2 * x + 1 + CO]
            other = jnp.where(lanes() % 2 == 0, pltpu.roll(tile, 127, 1), pltpu.roll(tile, 1, 1))
            tile = tile + other
            keep = inside[t] & row_inside(x, LX // 2)
            active = jnp.where(keep, 0.25 * jnp.broadcast_to(tile[6:7], (8, 128)), 0.0)
            kv[t, x + KO] = tile
            pairs_a.append(active)
            pairs_av.append(active * tile)
        keep_beside(ka, pairs_a, x + KO, 2)
        keep_beside(kav, pairs_av, x + KO, 2)

    def spread(field, low, high, spacing, shift, offset, flags, products, edges=True):
        weights_y, weights_z = factors(0.25 * spacing, 1), factors(0.5, 2)

        def body(x):
            r = x + offset
            if field is not None:
                here = [field[c, r] for c in range(4)]
                below, above = beside(here, shift, edges)
            for k, scale in enumerate((flags, products)):
                for c in range(4 if edges else 3):
                    near = [scale[j, c // 3, r] for j in range(3)]
                    if field is not None:
                        near = [near[0] * here[c], near[1] * below[c], near[2] * above[c]]
                    tile = near[0] + weights_y[c] * (near[1] + near[2])
                    g[k, c, r] = along_z(tile, weights_z[c])

        rows(low - 1, high + 1, body)

    def coupled(c, r, weights_x, flag, visc):
        p = g[0, c, r] + weights_x[c] * (g[0, c, r - 1] + g[0, c, r + 1])
        q = g[1, c, r] + weights_x[c] * (g[1, c, r - 1] + g[1, c, r + 1])
        return 2.0 * flag * (visc * p + q)

    def diagonals(low, high, spacing, ocean, shift, offset, flags, products, visc, diag, scaled):
        spread(None, low, high, spacing, shift, offset, flags, products)
        weights_x = factors(0.25 * spacing, 0)

        def body(x):
            r = x + offset
            for t in range(2):
                tile, flag, product = visc(t, x), flags[0, t, r], products[0, t, r]
                bottom = layers() == 0
                if t == 1:
                    bottom = bottom & (lanes() < 64)
                basal = jnp.where(bottom, jnp.broadcast_to(tile[7:8], (8, 128)), 0.0)
                base = REACTION * product + ocean * (1.0 - flag)
                for c in (3,) if t == 1 else range(3):
                    whole = coupled(c, r, weights_x, flag, tile) + base
                    if c != 2:
                        whole = whole + basal
                    diag[c, r] = whole
                    scaled[c, r] = DAMPING / (whole - 4.0 * flag * product)

        rows(low, high, body)

    def fine_visc(t, x):
        return cf[t, x + CO]

    def coarse_visc(t, x):
        return kv[t, x + KO]

    def fine_step(field, low, high, finish, edges=True):
        spread(field, low, high, 1.0, 1, FO, a, av, edges)
        weights_x = factors(0.25, 0)

        def body(x):
            r = x + FO
            for c in range(4 if edges else 3):
                flag, visc = a[0, c // 3, r], cf[c // 3, x + CO]
                value = field[c, r]
                left_over = f[c, r] - d[c, r] * value + coupled(c, r, weights_x, flag, visc)
                finish(c, x, value, left_over)

        rows(low, high, body)

    def smooth(field):
        def finish(c, x, value, left_over):
            field[c, x + FO] = value + inv[c, x + FO] * left_over

        return finish

    rows(-4, LX + 4, fine_fields)
    diagonals(-2, LX + 2, 1.0, 1.0, 1, FO, a, av, fine_visc, d, inv)
    for made in x_a:
        made.wait_send()
    fine_step(u, -2, LX + 2, smooth(u))
    fine_step(u, -1, LX + 1, smooth(u))

    spread(u, 0, LX, 1.0, 1, FO, a, av, False)
    fine_x = factors(0.25, 0)

    def restrict(X):
        for c in range(3):
            total = None
            for k in range(2):
                r = 2 * X + k + FO
                value = u[c, r]
                ub[c, r] = value
                part = coupled(c, r, fine_x, a[0, 0, r], cf[0, 2 * X + k + CO])
                part = f[c, r] - d[c, r] * value + part
                total = part if total is None else total + part
            other = jnp.where(lanes() % 2 == 0, pltpu.roll(total, 127, 1), pltpu.roll(total, 1, 1))
            kr[c, X + KO] = total + other

    rows(0, LX // 2, restrict)

    x_b = to_both_rows(tri(ub), FO, 3, LX)
    x_b += to_both_rows(tri(kr), KO, 5, LX // 2)

    def pack_b(ref, offset):
        def do(x, slot):
            pb[slot] = pack([ref[c, x + offset] for c in range(3)])

        return do

    def unpack_b(ref, offset):
        def do(x, slot):
            ref[3, x + offset] = edges_of(pbl[slot], pbr[slot])

        return do

    def own_b(do_u, do_k):
        def body(X):
            do_u(2 * X, 2 * X)
            do_u(2 * X + 1, 2 * X + 1)
            do_k(X, LX + X)

        rows(0, LX // 2, body)

    def halo_b(do_u, do_k):
        for j in range(3):
            do_u(j - 3, 24 + j)
            do_u(LX + j, 27 + j)
        for j in range(5):
            do_k(j - 5, 30 + j)
            do_k(LX // 2 + j, 35 + j)

    own_b(pack_b(ub, FO), pack_b(kr, KO))
    y_own_b = to_both_lanes(pb, pbl, pbr, 0, PACK_B_OWN)
    rows(-6, LX // 2 + 6, coarse_fields)
    for made in x_b:
        made.wait_recv()
    halo_b(pack_b(ub, FO), pack_b(kr, KO))
    y_halo_b = to_both_lanes(pb, pbl, pbr, PACK_B_OWN, PACK_B - PACK_B_OWN)
    diagonals(-5, LX // 2 + 5, 0.5, 4.0, 2, KO, ka, kav, coarse_visc, kd, kinv)
    for made in y_own_b:
        made.wait_recv()
    own_b(unpack_b(ub, FO), unpack_b(kr, KO))
    for made in y_halo_b:
        made.wait_recv()
    halo_b(unpack_b(ub, FO), unpack_b(kr, KO))

    def first_coarse(x):
        for c in range(4):
            kc[c, x + KO] = kinv[c, x + KO] * kr[c, x + KO]

    def coarse_step(low, high):
        spread(kc, low, high, 0.5, 2, KO, ka, kav)
        weights_x = factors(0.125, 0)

        def body(x):
            r = x + KO
            for c in range(4):
                flag, visc = ka[0, c // 3, r], kv[c // 3, r]
                value = kc[c, r]
                left_over = kr[c, r] - kd[c, r] * value
                left_over = left_over + coupled(c, r, weights_x, flag, visc)
                kc[c, r] = value + kinv[c, r] * left_over

        rows(low, high, body)

    half = LX // 2
    rows(-5, half + 5, first_coarse)
    coarse_step(-4, half + 4)
    coarse_step(-3, half + 3)
    coarse_step(-2, half + 2)

    def correct_row(x, X):
        for c in range(4):
            ub[c, x + FO] = ub[c, x + FO] + kc[c, X + KO]

    def correct(X):
        correct_row(2 * X, X)
        correct_row(2 * X + 1, X)

    for made in x_b:
        made.wait_send()
    rows(-1, half + 1, correct)
    correct_row(-3, -2)
    correct_row(LX + 2, half + 1)
    fine_step(ub, -2, LX + 2, smooth(ub))
    fine_step(ub, -1, LX + 1, smooth(ub))

    def finish(c, x, value, left_over):
        out_u[c, x] = value
        out_r[c, x] = left_over

    fine_step(ub, 0, LX, finish, False)

    for made in y_own + y_halo + y_own_b + y_halo_b:
        made.wait_send()


def shards(ntx, nty, forcing, start_state, ice_mask, class_ids, eta_table, friction):
    vmem = pl.BlockSpec(memory_space=pltpu.VMEM)

    def tiles(*lead):
        return pltpu.VMEM(lead + (8, 128), jnp.float32)

    out = jax.ShapeDtypeStruct((3, LX, 8, 128), jnp.float32)
    fine, coarse = tiles(4, FROWS), tiles(4, KROWS)
    hbm = pl.BlockSpec(memory_space=pltpu.HBM)
    adjoint, residual = pl.pallas_call(
        functools.partial(kernel, ntx, nty),
        out_shape=(out, out),
        in_specs=[hbm] * 6,
        out_specs=(vmem, vmem),
        scratch_shapes=[
            fine, fine, tiles(2, CROWS), tiles(3, 2, FROWS), tiles(3, 2, FROWS), fine, fine, fine,
            tiles(2, 4, FROWS), tiles(3, 2, KROWS), tiles(3, 2, KROWS), tiles(2, KROWS),
            coarse, coarse, coarse, coarse,
            tiles(PACK_A), tiles(PACK_A), tiles(PACK_A),
            tiles(PACK_B), tiles(PACK_B), tiles(PACK_B),
            pltpu.VMEM((3, NZ, LX, 128), jnp.float32), pltpu.VMEM((3, NZ, LX, 128), jnp.float32),
            pltpu.VMEM((NZ, LX, 128), jnp.int32), pltpu.VMEM((LX, 128), jnp.int32),
            pltpu.VMEM((LX, 128), jnp.float32), pltpu.SMEM((16,), jnp.float32),
            pltpu.SemaphoreType.DMA((18,)), pltpu.SemaphoreType.DMA((18,)), pltpu.SemaphoreType.DMA((6,)),
        ],
        compiler_params=pltpu.CompilerParams(
            collective_id=0, has_side_effects=True, vmem_limit_bytes=32 << 20
        ),
    )(*(
        pltpu.with_memory_space_constraint(value, pltpu.HBM)
        for value in (eta_table, forcing, start_state, ice_mask, class_ids, friction)
    ))

    def back(values):
        return jnp.transpose(values[:, :, :NZ], (0, 2, 1, 3))

    return back(adjoint), back(residual)


def solution(mesh):
    return jax.shard_map(
        functools.partial(shards, mesh.shape["tx"], mesh.shape["ty"]),
        mesh=mesh,
        in_specs=(
            P(None, None, "tx", "ty"),
            P(None, None, "tx", "ty"),
            P("tx", "ty"),
            P(None, "tx", "ty"),
            P(),
            P("tx", "ty"),
        ),
        out_specs=(P(None, None, "tx", "ty"), P(None, None, "tx", "ty")),
        check_vma=False,
    )
```
